32 devices in a mesh: dp: 4 (over z), mem: 8 (over y, x, core).
Axes of the slice: x: 2, y: 2, z: 4, core: 2. Of those that a mesh axis runs over, the one named last changes fastest.
Arguments:
- tokens: bfloat16 [4, 3072, 2048], P('dp')
- w_query: bfloat16 [2048, 2048], P(None, 'mem'), may hold values from -0.125 to 0.125
- w_key: bfloat16 [2048, 2048], P(None, 'mem'), may hold values from -0.125 to 0.125
- w_value: bfloat16 [2048, 2048], P(None, 'mem'), may hold values from -0.125 to 0.125
- gate_bias: float32 [16], P('mem'), may hold values from -2 to 2
- memory_keys: bfloat16 [4, 12288, 2048], P('dp', 'mem')
- memory_values: bfloat16 [4, 12288, 2048], P('dp', 'mem'), may hold values from -6 to 6
- retrieval_ids: int32 [4, 16, 24, 8], P('dp', 'mem'), may hold values from 0 to 191, as said below
- retrieval_counts: int32 [4, 16, 24], P('dp', 'mem'), may hold values from 1 to 8, as said below
- cotangent: bfloat16 [4, 3072, 2048], P('dp', None, 'mem')
Outputs:
- attended: bfloat16 [4, 3072, 2048], P('dp', None, 'mem')
- grad_q: float32 [2048, 2048], P('dp', 'mem')
- grad_k: float32 [2048, 2048], P('dp', 'mem')
- grad_v: float32 [2048, 2048], P('dp', 'mem')
- grad_gate: float32 [16], P('mem')
The draws below stay inside these ranges and needn't reach their ends.
Inputs may be any that keep to these rules, and one draw needn't show every extreme that they name: `retrieval_ids`: entry [d, h, b, j] names tile t of document d's memory, owned by index t // 24 of mem; only entries j < retrieval_counts[d, h, b] are live, the others are padding with arbitrary tile ids. Over the live entries of one head at most 24 name tiles of one owner, and in each document one owner is named by exactly 24 live entries of every head. `retrieval_counts`: the number of leading live entries of the list of block b of head h.
All inputs are finite; a program needn't handle non-finite values.
Results may differ from the reference program's by a relative error of at most 0.011.
Values may be sent and summed in bfloat16 or wider, within the bound.
A program may use at most 192 MiB of HBM per device.

```python
import jax
import jax.numpy as jnp
from jax import lax

D = 2048
HEADS = 16
DH = 128
SEG = 512
QB = 128
TILE = 64
TOP = 8
SEGS = 6
TILES_DEV = 24
DOCS = 4
TOK = 3072
NQB = 24
CAP = 24
MEM = 12288
TILES = 192


def retrieval_lists(key):
    base_key = jax.random.fold_in(key, 11)
    keys_all = jax.random.split(base_key, 8)
    slot_total = NQB * TOP
    owners_all = TILES // TILES_DEV
    spread = (owners_all - 1) * CAP
    hot_owner = jax.random.randint(keys_all[0], (DOCS, 1, 1), 0, owners_all)
    small_count = jax.random.randint(keys_all[1], (DOCS, HEADS, NQB), 1, 4)
    pick_full = jax.random.randint(keys_all[2], (DOCS, HEADS, NQB), 0, 4) == 0
    forced = jax.random.randint(keys_all[3], (DOCS, 1, 1), 0, HEADS * NQB)
    flat_index = jnp.arange(HEADS * NQB).reshape(1, HEADS, NQB)
    counts = jnp.where(pick_full | (flat_index == forced), TOP, small_count).astype(jnp.int32)
    live_slot = (jnp.arange(TOP)[None, None, None, :] < counts[..., None]).reshape(DOCS, HEADS, slot_total)
    order_score = jax.random.randint(keys_all[4], (DOCS, HEADS, slot_total), 0, slot_total) * slot_total + jnp.arange(slot_total)
    order_score = jnp.where(live_slot, order_score, order_score + slot_total * slot_total)
    slot_order = jnp.argsort(order_score, axis=-1, stable=True)
    position = jnp.argsort(slot_order, axis=-1, stable=True)
    spread_base = jnp.arange(spread)[None, None, :] // CAP
    other_owner = spread_base + (spread_base >= hot_owner).astype(jnp.int32)
    other_owner = jnp.broadcast_to(other_owner, (DOCS, HEADS, spread))
    mix_score = jax.random.randint(keys_all[5], (DOCS, HEADS, spread), 0, spread) * spread + jnp.arange(spread)
    mix_order = jnp.argsort(mix_score, axis=-1, stable=True)
    other_seq = jnp.take_along_axis(other_owner, mix_order, axis=-1)
    rest_index = jnp.clip(position - CAP, 0, spread - 1)
    rest_owner = jnp.take_along_axis(other_seq, rest_index, axis=-1)
    live_owner = jnp.where(position < CAP, hot_owner, rest_owner)
    pad_owner = jax.random.randint(keys_all[6], (DOCS, HEADS, slot_total), 0, owners_all)
    owner_id = jnp.where(live_slot, live_owner, pad_owner)
    local_tile = jax.random.randint(keys_all[7], (DOCS, HEADS, slot_total), 0, TILES_DEV)
    tile_ids = (owner_id * TILES_DEV + local_tile).reshape(DOCS, HEADS, NQB, TOP).astype(jnp.int32)
    return (tile_ids, counts)


def draw_retrieval_ids(key, part):
    return retrieval_lists(key)[0]


def draw_retrieval_counts(key, part):
    return retrieval_lists(key)[1]


def draw_tokens(key, part):
    shape_all = (DOCS, TOK, D)
    values = jax.random.normal(key, shape_all, jnp.float32)
    return values.astype(jnp.bfloat16)


def draw_memory_keys(key, part):
    shape_all = (DOCS, TILES, TILE, HEADS * DH)
    values = jax.random.normal(key, shape_all, jnp.float32)
    return values.reshape(DOCS, MEM, HEADS * DH).astype(jnp.bfloat16)


def draw_cotangent(key, part):
    shape_all = (DOCS, TOK, HEADS * DH)
    position = jnp.arange(DOCS, dtype=jnp.float32)[:, None, None] / (DOCS - 1)
    scaling = (DOCS * TOK) ** (-0.5)
    values = jax.random.normal(key, shape_all, jnp.float32) * (1.0 + 2.0 * position)
    return (values * scaling).astype(jnp.bfloat16)


def block_scale(rng, extent, pieces, low, high):
    gain = 1.0
    for axis_at, shards_of in pieces:
        draws = jax.random.uniform(jax.random.fold_in(jax.random.fold_in(rng, 6), axis_at), (shards_of,), jnp.float32, low / len(pieces), high / len(pieces))
        gain = gain * jnp.repeat(jnp.exp(draws), extent[axis_at] // shards_of).reshape((-1,) + (1,) * (len(extent) - 1 - axis_at))
    return gain


def bell_draw(rng, extent, scale, bound, cuts=(), held_as=jnp.bfloat16):
    array = jax.random.normal(rng, extent, jnp.float32) * scale
    if len(cuts) > 0:
        array = block_scale(rng, extent, cuts, -0.22, 0.18) * array
    return jnp.clip(array, min=-bound, max=bound).astype(held_as)


def setup_inputs(seed: int = 0) -> dict:
    streams_of = jax.random.split(jax.random.key(seed), 11)
    tokens = draw_tokens(jax.random.fold_in(streams_of[10], 71), 0)
    w_query = bell_draw(streams_of[1], (D, HEADS * DH), D ** -0.5, 0.125, ((1, 8),))
    w_key = bell_draw(streams_of[2], (D, HEADS * DH), D ** -0.5, 0.125, ((1, 8),))
    w_value = bell_draw(streams_of[3], (D, HEADS * DH), D ** -0.5, 0.125, ((1, 8),))
    gate_bias = jnp.clip(jax.random.uniform(streams_of[4], (HEADS,), jnp.float32, -2.0, 2.0) * block_scale(streams_of[4], (HEADS,), ((0, 8),), -0.4, 0.0), -2.0, 2.0)
    memory_keys = draw_memory_keys(jax.random.fold_in(streams_of[10], 71), 0)
    memory_values = bell_draw(streams_of[6], (DOCS, MEM, HEADS * DH), 1.0, 6.0, ((0, 4), (1, 8)))
    retrieval_ids = draw_retrieval_ids(jax.random.fold_in(streams_of[10], 71), 0)
    retrieval_counts = draw_retrieval_counts(jax.random.fold_in(streams_of[10], 71), 0)
    cotangent = draw_cotangent(jax.random.fold_in(streams_of[10], 71), 0)
    return {"tokens": tokens, "w_query": w_query, "w_key": w_key, "w_value": w_value, "gate_bias": gate_bias, "memory_keys": memory_keys, "memory_values": memory_values, "retrieval_ids": retrieval_ids, "retrieval_counts": retrieval_counts, "cotangent": cotangent}


def rounded(values):
    return lax.optimization_barrier(values.astype(jnp.bfloat16)).astype(jnp.float32)


def split_heads(matrix):
    return matrix.reshape(matrix.shape[0], HEADS, DH).transpose(1, 0, 2)


def join_heads(stacked):
    return stacked.transpose(1, 0, 2).reshape(stacked.shape[1], HEADS * DH)


def softmax_rows(scores):
    largest = jnp.max(scores, axis=-1, keepdims=True)
    raised = jnp.exp(scores - largest)
    return raised / jnp.sum(raised, axis=-1, keepdims=True)


def back_softmax(soft_rows, grad_rows, scaling):
    return soft_rows * (grad_rows - jnp.sum(grad_rows * soft_rows, axis=-1, keepdims=True)) * scaling


def reference(tokens, w_query, w_key, w_value, gate_bias, memory_keys, memory_values, retrieval_ids, retrieval_counts, cotangent):
    scaling = DH ** -0.5
    causal = jnp.arange(SEG)[:, None] >= jnp.arange(SEG)[None, :]
    gate = jax.nn.sigmoid(gate_bias.astype(jnp.float32))
    gate_col = gate[:, None, None]
    head_index = jnp.arange(HEADS)[:, None, None]

    def one_document(carry, inputs):
        hidden, mem_keys, mem_values, tile_ids, counts, upstream_in = inputs
        queries = split_heads(jnp.dot(hidden, w_query, preferred_element_type=jnp.float32).astype(jnp.bfloat16))
        keys_local = split_heads(jnp.dot(hidden, w_key, preferred_element_type=jnp.float32).astype(jnp.bfloat16))
        values_local = split_heads(jnp.dot(hidden, w_value, preferred_element_type=jnp.float32).astype(jnp.bfloat16))
        seg_queries = queries.reshape(HEADS, SEGS, SEG, DH).astype(jnp.float32)
        seg_keys = keys_local.reshape(HEADS, SEGS, SEG, DH).astype(jnp.float32)
        seg_values = values_local.reshape(HEADS, SEGS, SEG, DH).astype(jnp.float32)
        local_scores = jnp.einsum("hnqe,hnke->hnqk", seg_queries, seg_keys) * scaling
        local_probs = softmax_rows(jnp.where(causal, local_scores, -jnp.inf))
        local_round = rounded(local_probs)
        local_out = jnp.einsum("hnqk,hnke->hnqe", local_round, seg_values).reshape(HEADS, TOK, DH)
        key_tiles = mem_keys.reshape(TILES, TILE, HEADS, DH)[tile_ids, :, head_index]
        key_tiles = key_tiles.reshape(HEADS, NQB, TOP * TILE, DH).astype(jnp.float32)
        value_tiles = mem_values.reshape(TILES, TILE, HEADS, DH)[tile_ids, :, head_index]
        value_tiles = value_tiles.reshape(HEADS, NQB, TOP * TILE, DH).astype(jnp.float32)
        live_slot = jnp.arange(TOP)[None, None, :] < counts[:, :, None]
        live_keys = jnp.repeat(live_slot, TILE, axis=2)[:, :, None, :]
        block_queries = queries.reshape(HEADS, NQB, QB, DH).astype(jnp.float32)
        mem_scores = jnp.einsum("hbqe,hbke->hbqk", block_queries, key_tiles) * scaling
        mem_probs = softmax_rows(jnp.where(live_keys, mem_scores, -jnp.inf))
        mem_round = rounded(mem_probs)
        mem_out = jnp.einsum("hbqk,hbke->hbqe", mem_round, value_tiles).reshape(HEADS, TOK, DH)
        attended = join_heads((gate_col * mem_out + (1.0 - gate_col) * local_out).astype(jnp.bfloat16))
        upstream = split_heads(upstream_in).astype(jnp.float32)
        gate_term = jnp.sum(upstream * (mem_out - local_out), axis=(1, 2)) * gate * (1.0 - gate)
        grad_mem = rounded(gate_col * upstream)
        grad_local = rounded((1.0 - gate_col) * upstream)
        mem_grad_rows = jnp.einsum("hbqe,hbke->hbqk", grad_mem.reshape(HEADS, NQB, QB, DH), value_tiles)
        mem_dround = rounded(back_softmax(mem_probs, mem_grad_rows, scaling))
        mem_dq = jnp.einsum("hbqk,hbke->hbqe", mem_dround, key_tiles).reshape(HEADS, TOK, DH)
        seg_grad = grad_local.reshape(HEADS, SEGS, SEG, DH)
        local_grad_rows = jnp.einsum("hnqe,hnke->hnqk", seg_grad, seg_values)
        local_dround = rounded(back_softmax(local_probs, local_grad_rows, scaling))
        local_dq = jnp.einsum("hnqk,hnke->hnqe", local_dround, seg_keys).reshape(HEADS, TOK, DH)
        grad_queries = (mem_dq + local_dq).astype(jnp.bfloat16)
        grad_keys = jnp.einsum("hnqk,hnqe->hnke", local_dround, seg_queries).astype(jnp.bfloat16).reshape(HEADS, TOK, DH)
        grad_values = jnp.einsum("hnqk,hnqe->hnke", local_round, seg_grad).astype(jnp.bfloat16).reshape(HEADS, TOK, DH)
        weight_q = jnp.dot(hidden.T, join_heads(grad_queries), preferred_element_type=jnp.float32)
        weight_k = jnp.dot(hidden.T, join_heads(grad_keys), preferred_element_type=jnp.float32)
        weight_v = jnp.dot(hidden.T, join_heads(grad_values), preferred_element_type=jnp.float32)
        carry = (carry[0] + weight_q, carry[1] + weight_k, carry[2] + weight_v, carry[3] + gate_term)
        return carry, attended

    zero_weight = jnp.zeros((D, HEADS * DH), jnp.float32)
    start = (zero_weight, zero_weight, zero_weight, jnp.zeros((HEADS,), jnp.float32))
    totals, attended = lax.scan(one_document, start, (tokens, memory_keys, memory_values, retrieval_ids, retrieval_counts, cotangent))
    return (attended, totals[0], totals[1], totals[2], totals[3])
```

```python
import functools

import jax
import jax.numpy as jnp
from jax import lax
from jax.experimental import pallas as pl
from jax.experimental.pallas import tpu as pltpu
from jax.sharding import PartitionSpec as P

DH = 128
SEG = 512
QB = 128
TILE = 64
ROWS = 256
PAIR = 2
LANES = 128
OVER = 120
BAD = 121
NEG = -1e30
F32 = jnp.float32
BF16 = jnp.bfloat16
I32 = jnp.int32
MESH = pl.DeviceIdType.MESH


def dot_nn(a, b):
    return lax.dot_general(a, b, (((1,), (0,)), ((), ())), preferred_element_type=F32)


def dot_nt(a, b):
    return lax.dot_general(a, b, (((1,), (1,)), ((), ())), preferred_element_type=F32)


def dot_tn(a, b):
    return lax.dot_general(a, b, (((0,), (0,)), ((), ())), preferred_element_type=F32)


def softmax_rows(scores):
    raised = jnp.exp(scores - jnp.max(scores, axis=-1, keepdims=True))
    return raised * (1.0 / jnp.sum(raised, axis=-1, keepdims=True))


def back_softmax(probs, grad_rows, scaling):
    return (
        probs * (grad_rows - jnp.sum(grad_rows * probs, axis=-1, keepdims=True)) * scaling
    ).astype(BF16)


def from_others(pick):
    count = lax.axis_size("dp")
    me = lax.axis_index("dp")
    got = []
    for shift in range(1, count):
        pairs = [(i, (i + shift) % count) for i in range(count)]
        got.append(lax.ppermute(pick((me + shift) % count), "dp", pairs))
    return got


def exchange_rows(term):
    rows = term.shape[0] // lax.axis_size("dp")

    def pick(owner):
        return lax.dynamic_slice_in_dim(term, owner * rows, rows, 0)

    return [pick(lax.axis_index("dp"))] + from_others(pick)


def add_rows(blocks):
    total = blocks[0].astype(F32)
    for got in blocks[1:]:
        total += got.astype(F32)
    return total


def to_owners(packed):
    return lax.all_to_all(packed, "mem", split_axis=0, concat_axis=0, tiled=True)


def iota(shape, dim):
    return lax.broadcasted_iota(I32, shape, dim).astype(F32)


def plan_kernel(owners, tiles_dev, top, first, second, lists_ref, rows_ref, at_ref):
    heads, blocks, _ = lists_ref.shape
    tiles = owners * tiles_dev

    def group_of(tile):
        return jnp.floor((tile + 0.5) * (1.0 / tiles_dev))

    def neighbour(group):
        return group + 1.0 - 2.0 * (group - 2.0 * jnp.floor(group * 0.5 + 0.25))

    tile_row = iota((1, tiles), 1)
    owner_row = group_of(tile_row)
    other_row = neighbour(owner_row)
    local_row = tile_row - owner_row * tiles_dev
    square_a, square_b = iota((tiles, tiles), 0), iota((tiles, tiles), 1)
    group_a, group_b = group_of(square_a), group_of(square_b)
    same = group_a == group_b
    as_f32 = lambda mask: jnp.where(mask, 1.0, 0.0)
    before = as_f32(same & (square_a < square_b))
    whole = as_f32(same)
    across = as_f32(group_a == neighbour(group_b))
    slot_tile = iota((blocks, tiles), 1)
    named, hits = [], []
    for h in range(heads):
        entries = lists_ref[h]
        count = entries[:, top : top + 1]
        hits.append([slot_tile == entries[:, j : j + 1].astype(F32) for j in range(top)])
        flag = jnp.zeros((blocks, tiles), F32)
        for j in range(top):
            flag = jnp.maximum(flag, jnp.where(hits[h][j] & (count > j), 1.0, 0.0))
        named.append(jnp.max(flag, axis=0, keepdims=True))
    eight = lambda row: jnp.broadcast_to(row, (8, tiles))
    start = jnp.zeros((1, tiles), F32)
    theirs = jnp.zeros((1, tiles), F32)
    ranks = []
    for h in range(heads):
        flags = eight(named[h])
        ranks.append(start + dot_nn(flags, before)[:1])
        start = start + dot_nn(flags, whole)[:1]
        theirs = theirs + dot_nn(flags, across)[:1]
        if h == 0:
            head_count = start
    over = jnp.maximum(theirs - (first + second), 0.0)
    mine = jnp.minimum(jnp.maximum(start - first, 0.0), float(second))
    bad = (head_count > first) | (start > first + 2 * second) | (mine + over > second)
    bad = jnp.max(as_f32(bad))

    lane = iota((LANES, tiles), 0)
    rank_of = jnp.where(
        lane < first + second, lane, float(2 * first + 3 * second - 1) - lane
    )
    owner_col = iota((owners, tiles), 0)
    mine_of = owner_col == owner_row
    rows = jnp.zeros((owners, LANES), F32)
    for h in range(heads):
        chosen = as_f32((rank_of == ranks[h]) & (lane < first + 2 * second)) * named[h]
        codes = jnp.where(mine_of, local_row + float(h * tiles_dev), 0.0)
        rows = rows + dot_nt(codes, chosen)
    over_col = jnp.sum(jnp.where(mine_of & (local_row == 0.0), over, 0.0), axis=1, keepdims=True)
    at_lane = iota((owners, LANES), 1)
    rows = jnp.where(at_lane == OVER, over_col, rows)
    rows = jnp.where(at_lane == BAD, bad, rows)
    rows_ref[:, 0, :] = rows.astype(I32)

    slot_lane = iota((blocks, top), 1)
    for h in range(heads):
        rank = ranks[h]
        place = jnp.where(
            rank < first,
            owner_row * first + rank,
            jnp.where(
                rank < first + second,
                owners * first + owner_row * second + rank - first,
                owners * first + other_row * second + (first + 2 * second - 1) - rank,
            ),
        )
        count = lists_ref[h][:, top : top + 1]
        at = jnp.zeros((blocks, top), F32)
        for j in range(top):
            found = jnp.sum(jnp.where(hits[h][j], place, 0.0), axis=1, keepdims=True)
            if j == 0:
                lead = found
            at = jnp.where(slot_lane == j, jnp.where(count > j, found, lead), at)
        at_ref[h] = at.astype(I32)


def plan(ids, counts, owners, tiles_dev, first, second):
    heads, blocks, top = ids.shape
    lists = jnp.concatenate([ids, counts[..., None]], axis=-1)
    return pl.pallas_call(
        functools.partial(plan_kernel, owners, tiles_dev, top, first, second),
        name="plan",
        out_shape=[
            jax.ShapeDtypeStruct((owners, 1, LANES), I32),
            jax.ShapeDtypeStruct((heads, blocks, top), I32),
        ],
    )(lists)


def swap_kernel(docs, owners, rows_ref, got_ref, bad_ref, land, flags, send_sem, recv_sem):
    doc, me = lax.axis_index("dp"), lax.axis_index("mem")
    barrier = pltpu.get_barrier_semaphore()
    flags[...] = jnp.zeros_like(flags)
    peers = []
    for away in range(docs):
        for step in range(owners):
            if away or step:
                peers.append((away, step, lax.rem(doc + away, docs), lax.rem(me + step, owners)))
    for _, _, d, m in peers:
        pl.semaphore_signal(barrier, inc=1, device_id=(d, m), device_id_type=MESH)
    pl.semaphore_wait(barrier, len(peers))
    copies = []
    for n, (away, step, d, m) in enumerate(peers):
        copies.append(
            pltpu.make_async_remote_copy(
                src_ref=rows_ref.at[0] if away else rows_ref.at[m],
                dst_ref=flags.at[away * owners + step] if away else land.at[step],
                send_sem=send_sem.at[n],
                recv_sem=recv_sem.at[n],
                device_id=(d, m),
                device_id_type=MESH,
            )
        )
        copies[-1].start()
    got_ref[me] = rows_ref[me]
    for copy in copies:
        copy.wait()
    for step in range(1, owners):
        got_ref[lax.rem(me + owners - step, owners)] = land[step]
    worst = jnp.max(flags[...], axis=0)
    for step in range(1, owners):
        worst = jnp.maximum(worst, land[step])
    bad_ref[...] = jnp.maximum(worst, rows_ref[0])


def swap(rows, docs):
    owners = rows.shape[0]
    vmem = pl.BlockSpec(memory_space=pltpu.VMEM)
    count = docs * owners
    return pl.pallas_call(
        functools.partial(swap_kernel, docs, owners),
        name="swap",
        in_specs=[vmem],
        out_specs=[vmem, vmem],
        out_shape=[
            jax.ShapeDtypeStruct((owners, 1, LANES), I32),
            jax.ShapeDtypeStruct((1, LANES), I32),
        ],
        scratch_shapes=[
            pltpu.VMEM((owners, 1, LANES), I32),
            pltpu.VMEM((count, 1, LANES), I32),
            pltpu.SemaphoreType.DMA((count,)),
            pltpu.SemaphoreType.DMA((count,)),
        ],
        compiler_params=pltpu.CompilerParams(collective_id=0, has_side_effects=True),
    )(rows)


def pack_kernel(heads, tiles_dev, base, parts, codes_ref, keys_ref, values_ref, *rest):
    outs, buf, in_sem, out_sem = rest[: len(parts)], rest[-3], rest[-2], rest[-1]
    owners, slots = buf.shape[0], buf.shape[1]

    for d in range(owners):

        def fetch(c, carry, d=d):
            code = codes_ref[d * LANES + base + c]
            head = code // tiles_dev
            tile = code - head * tiles_dev
            rows = pl.ds(pl.multiple_of(tile * TILE, TILE), TILE)
            cols = pl.ds(pl.multiple_of((d * heads + head) * DH, DH), DH)
            pltpu.make_async_copy(keys_ref.at[rows, cols], buf.at[d, c, 0], in_sem.at[d]).start()
            pltpu.make_async_copy(values_ref.at[rows, cols], buf.at[d, c, 1], in_sem.at[d]).start()
            return carry

        lax.fori_loop(0, slots, fetch, 0, unroll=2)
    copies = []
    for d in range(owners):
        pltpu.make_async_copy(buf.at[d], buf.at[d], in_sem.at[d]).wait()
        at = 0
        for n, (out, count) in enumerate(zip(outs, parts)):
            copies.append(
                pltpu.make_async_copy(
                    buf.at[d, at : at + count], out.at[d], out_sem.at[d, n]
                )
            )
            copies[-1].start()
            at += count
    for copy in copies:
        copy.wait()


def pack(codes, keys, values, owners, heads, tiles_dev, base, parts):
    keep = pl.BlockSpec(memory_space=pl.ANY)
    slots = sum(parts)
    return pl.pallas_call(
        functools.partial(pack_kernel, heads, tiles_dev, base, parts),
        name=f"pack_{base}",
        grid_spec=pltpu.PrefetchScalarGridSpec(
            num_scalar_prefetch=1,
            grid=(1,),
            in_specs=[keep, keep],
            out_specs=[keep] * len(parts),
            scratch_shapes=[
                pltpu.VMEM((owners, slots, 2, TILE, DH), BF16),
                pltpu.SemaphoreType.DMA((owners,)),
                pltpu.SemaphoreType.DMA((owners, len(parts))),
            ],
        ),
        out_shape=[jax.ShapeDtypeStruct((owners, n, 2, TILE, DH), BF16) for n in parts],
        compiler_params=pltpu.CompilerParams(vmem_limit_bytes=24 << 20),
        cost_estimate=pl.CostEstimate(
            flops=0, bytes_accessed=8 * owners * slots * TILE * DH, transcendentals=0
        ),
    )(codes, keys, values)


def rearrange_kernel(keys_ref, values_ref, out_ref):
    tiles_dev = out_ref.shape[1]
    out_ref[0, :, 0] = keys_ref[...].reshape(tiles_dev, TILE, DH)
    out_ref[0, :, 1] = values_ref[...].reshape(tiles_dev, TILE, DH)


def rearrange(mem_keys, mem_values, head, heads_here, mem_devices):
    rows = mem_keys.shape[0]
    tiles_dev = rows // TILE
    column = pl.BlockSpec((rows, DH), lambda d: (0, d * heads_here + head))
    return pl.pallas_call(
        rearrange_kernel,
        name=f"rearrange_{head}",
        grid=(mem_devices,),
        in_specs=[column, column],
        out_specs=pl.BlockSpec((1, tiles_dev, 2, TILE, DH), lambda d: (d, 0, 0, 0, 0)),
        out_shape=jax.ShapeDtypeStruct((mem_devices, tiles_dev, 2, TILE, DH), BF16),
        compiler_params=pltpu.CompilerParams(vmem_limit_bytes=56 << 20),
        cost_estimate=pl.CostEstimate(
            flops=0, bytes_accessed=8 * mem_devices * rows * DH, transcendentals=0
        ),
    )(mem_keys, mem_values)


def local_kernel(
    heads, gate_ref, x_ref, wq_ref, wk_ref, wv_ref, cot_ref, q_ref, lo_ref, dq_ref, w_ref, acc_ref
):
    step = pl.program_id(0)
    scaling = DH ** (-0.5)
    x = x_ref[...]
    q = dot_nn(x, wq_ref[...]).astype(BF16)
    k = dot_nn(x, wk_ref[...]).astype(BF16)
    v = dot_nn(x, wv_ref[...]).astype(BF16)
    q_ref[...] = q
    all_dk, all_dv = [], []
    for h in range(heads):
        cols = slice(h * DH, (h + 1) * DH)
        qh, kh, vh = q[:, cols], k[:, cols], v[:, cols]
        up = cot_ref[:, cols].astype(F32)
        gl = ((1.0 - gate_ref[h]) * up).astype(BF16)
        dk = [None] * (SEG // ROWS)
        dv = [None] * (SEG // ROWS)
        for i in range(SEG // ROWS):
            n = (i + 1) * ROWS
            rows = slice(i * ROWS, n)
            s = dot_nt(qh[rows], kh[:n]) * scaling
            at_q = lax.broadcasted_iota(jnp.int32, (ROWS, n), 0) + i * ROWS
            at_k = lax.broadcasted_iota(jnp.int32, (ROWS, n), 1)
            p = softmax_rows(jnp.where(at_q >= at_k, s, NEG))
            pr = p.astype(BF16)
            lo_ref[rows, cols] = dot_nn(pr, vh[:n])
            ds = back_softmax(p, dot_nt(gl[rows], vh[:n]), scaling)
            dq_ref[rows, cols] = dot_nn(ds, kh[:n])
            for j in range(i + 1):
                part = slice(j * ROWS, (j + 1) * ROWS)
                tk = dot_tn(ds[:, part], qh[rows])
                tv = dot_tn(pr[:, part], gl[rows])
                dk[j] = tk if dk[j] is None else dk[j] + tk
                dv[j] = tv if dv[j] is None else dv[j] + tv
        all_dk.append(jnp.concatenate(dk, axis=0).astype(BF16))
        all_dv.append(jnp.concatenate(dv, axis=0).astype(BF16))
    grads = jnp.concatenate(all_dk + all_dv, axis=1)
    term = dot_tn(x, grads)

    @pl.when(step == 0)
    def _():
        acc_ref[...] = term

    @pl.when(step > 0)
    def _():
        acc_ref[...] += term

    @pl.when(step == pl.num_programs(0) - 1)
    def _():
        w_ref[...] = acc_ref[...].astype(BF16)


def local_part(hidden, w_query, w_key, w_value, gate, cotangent, heads):
    tok, d = hidden.shape
    width = heads * DH
    rows = pl.BlockSpec((SEG, width), lambda s: (s, 0))
    weight = pl.BlockSpec((d, width), lambda s: (0, 0), pipeline_mode=pl.Buffered(1))
    return pl.pallas_call(
        functools.partial(local_kernel, heads),
        name="local_part",
        grid=(tok // SEG,),
        in_specs=[
            pl.BlockSpec(memory_space=pltpu.SMEM),
            pl.BlockSpec((SEG, d), lambda s: (s, 0)),
            weight,
            weight,
            weight,
            rows,
        ],
        out_specs=[rows, rows, rows, pl.BlockSpec((d, 2 * width), lambda s: (0, 0))],
        out_shape=[
            jax.ShapeDtypeStruct((tok, width), BF16),
            jax.ShapeDtypeStruct((tok, width), F32),
            jax.ShapeDtypeStruct((tok, width), F32),
            jax.ShapeDtypeStruct((d, 2 * width), BF16),
        ],
        scratch_shapes=[pltpu.VMEM((d, 2 * width), F32)],
        compiler_params=pltpu.CompilerParams(vmem_limit_bytes=56 << 20),
        cost_estimate=pl.CostEstimate(
            flops=20 * tok * d * width, bytes_accessed=2 * tok * d, transcendentals=0
        ),
    )(gate, hidden, w_query, w_key, w_value, cotangent)


def memory_kernel(
    head, top, parts, ids_ref, counts_ref, gate_ref, q_ref, cot_ref, lo_ref, dq_ref, *rest
):
    stores = rest[:parts]
    att_ref, gq_ref, sum_ref, kv_ref, sem = rest[-5:]
    step = pl.program_id(0)
    scaling = DH ** (-0.5)
    gate = gate_ref[head]

    @pl.when(step == 0)
    def _():
        sum_ref[...] = jnp.zeros_like(sum_ref)
        copies = []
        at = 0
        for n, store in enumerate(stores):
            into = kv_ref.at[at : at + store.shape[0]]
            copies.append(pltpu.make_async_copy(store, into, sem.at[n]))
            copies[-1].start()
            at += store.shape[0]
        for copy in copies:
            copy.wait()

    def run(slots):
        width = slots * TILE
        for u in range(PAIR):
            rows = slice(u * QB, (u + 1) * QB)
            block = step * PAIR + u
            q = q_ref[rows, :]
            up = cot_ref[rows, :].astype(F32)
            lo = lo_ref[rows, :]
            gm = (gate * up).astype(BF16)
            at = [ids_ref[block * top + j] for j in range(slots)]
            k = jnp.concatenate([kv_ref[t, 0] for t in at], axis=0)
            v = jnp.concatenate([kv_ref[t, 1] for t in at], axis=0)
            live = counts_ref[block] * TILE
            s = dot_nt(q, k) * scaling
            col = lax.broadcasted_iota(jnp.int32, (QB, width), 1)
            p = softmax_rows(jnp.where(col < live, s, NEG))
            mo = dot_nn(p.astype(BF16), v)
            ds = back_softmax(p, dot_nt(gm, v), scaling)
            gq_ref[rows, :] = (dot_nn(ds, k) + dq_ref[rows, :]).astype(BF16)
            att_ref[rows, :] = (gate * mo + (1.0 - gate) * lo).astype(BF16)
            sum_ref[...] += jnp.sum((up * (mo - lo)).reshape(QB // 8, 8, DH), axis=0)

    longest = counts_ref[step * PAIR]
    for u in range(1, PAIR):
        longest = jnp.maximum(longest, counts_ref[step * PAIR + u])
    half = top // 2

    @pl.when(longest <= half)
    def _():
        run(half)

    @pl.when(longest > half)
    def _():
        run(top)


def memory_part(head, at, counts, gate, q, cotangent, lo, dq, stores, earlier):
    tok, width = q.shape
    top = at.shape[1]
    stores = [kv.reshape(-1, 2, TILE, DH) for kv in stores]
    tiles = sum(kv.shape[0] for kv in stores)
    block = pl.BlockSpec((PAIR * QB, DH), lambda b, *_: (b, head))
    keep = pl.BlockSpec(memory_space=pl.ANY)
    return pl.pallas_call(
        functools.partial(memory_kernel, head, top, len(stores)),
        name=f"memory_part_{head}",
        grid_spec=pltpu.PrefetchScalarGridSpec(
            num_scalar_prefetch=3,
            grid=(tok // (PAIR * QB),),
            in_specs=[block, block, block, block] + [keep] * (len(stores) + len(earlier)),
            out_specs=[
                block,
                pl.BlockSpec((PAIR * QB, DH), lambda b, *_: (b, 0)),
                pl.BlockSpec((8, DH), lambda b, *_: (0, 0)),
            ],
            scratch_shapes=[
                pltpu.VMEM((tiles, 2, TILE, DH), BF16),
                pltpu.SemaphoreType.DMA((len(stores),)),
            ],
        ),
        out_shape=[
            jax.ShapeDtypeStruct((tok, width), BF16),
            jax.ShapeDtypeStruct((tok, DH), BF16),
            jax.ShapeDtypeStruct((8, DH), F32),
        ],
        input_output_aliases={7 + len(stores) + i: i for i in range(len(earlier))},
        compiler_params=pltpu.CompilerParams(vmem_limit_bytes=56 << 20),
        cost_estimate=pl.CostEstimate(
            flops=8 * tok * top * TILE * DH,
            bytes_accessed=4 * tiles * TILE * DH,
            transcendentals=0,
        ),
    )(at.reshape(-1), counts, gate, q, cotangent, lo, dq, *stores, *earlier)


def layer(local, fetch, heads):
    hidden, weights, gate, cot, counts = local
    stores, at, later = fetch
    width = heads * DH
    q, lo, dq, weight_kv = local_part(hidden, *weights, gate, cot, heads)
    stores, q = later(stores, q)
    blocks_kv = exchange_rows(weight_kv)
    earlier = ()
    sums = []
    shares_q = []
    for h in range(heads):
        attended, grad_q, total = memory_part(
            h, at[h], counts[h], gate, q, cot, lo, dq, stores[h], earlier
        )
        earlier = (attended,)
        sums.append(jnp.sum(total))
        weight_q = jnp.einsum("td,tf->df", hidden, grad_q, preferred_element_type=F32)
        blocks_q = exchange_rows(weight_q.astype(BF16))
        if h == 0:
            grad_q, blocks_kv = lax.optimization_barrier((grad_q, blocks_kv))
            share_kv = add_rows(blocks_kv)
        if h + 1 < heads:
            last, blocks_q = lax.optimization_barrier((stores[h + 1][-1], blocks_q))
            stores[h + 1] = stores[h + 1][:-1] + [last]
        shares_q.append(add_rows(blocks_q))
    share_q = jnp.concatenate(shares_q, axis=1)
    gate_term = jnp.stack(sums) * gate * (1.0 - gate)
    grad_gate = gate_term
    for got in from_others(lambda owner: gate_term):
        grad_gate += got
    return attended, share_q, share_kv[:, :width], share_kv[:, width:], grad_gate


def on_device(
    tokens,
    w_query,
    w_key,
    w_value,
    gate_bias,
    memory_keys,
    memory_values,
    retrieval_ids,
    retrieval_counts,
    cotangent,
):
    heads = gate_bias.shape[0]
    owners = lax.axis_size("mem")
    keys, values = memory_keys[0], memory_values[0]
    ids, counts = retrieval_ids[0], retrieval_counts[0]
    tiles_dev = keys.shape[0] // TILE
    gate = jax.nn.sigmoid(gate_bias)
    local = (tokens[0], (w_query, w_key, w_value), gate, cotangent[0], counts)

    def dense():
        sent = [rearrange(keys, values, h, heads, owners) for h in range(heads)]

        def later(stores, q):
            for h in range(1, heads):
                tied, q = lax.optimization_barrier((sent[h], q))
                stores.append([to_owners(tied)])
            return stores, q

        return layer(local, ([[to_owners(sent[0])]], ids, later), heads)

    first, second = tiles_dev * 5 // 6, tiles_dev * 3 // 8
    if heads != 2 or owners % 2 or first + 2 * second > OVER:
        out = dense()
    else:
        rows, at = plan(ids, counts, owners, tiles_dev, first, second)
        got, bad = swap(rows, lax.axis_size("dp"))

        def sparse():
            codes = got.reshape(-1)
            (chunk,) = pack(codes, keys, values, owners, heads, tiles_dev, 0, (first,))
            codes, chunk = lax.optimization_barrier((codes, chunk))
            one = to_owners(chunk)
            own, lent = pack(
                codes, keys, values, owners, heads, tiles_dev, first, (second, second)
            )
            pairs = [(i, i ^ 1) for i in range(owners)]
            borrowed = lax.ppermute(lent, "mem", pairs)
            room = second - got[:, 0, OVER]
            use_own = (jnp.arange(second)[None, :] < room[:, None])[:, :, None, None, None]

            def later(stores, q):
                merged = jnp.where(use_own, own, borrowed)
                tied, q = lax.optimization_barrier((merged, q))
                return stores + [[one, to_owners(tied)]], q

            return layer(local, ([[one]], at, later), heads)

        out = lax.cond(bad[0, BAD] == 0, sparse, dense)
    attended, share_q, share_k, share_v, grad_gate = out
    return attended[None], share_q, share_k, share_v, grad_gate


def solution(mesh):
    return jax.shard_map(
        on_device,
        mesh=mesh,
        in_specs=(
            P("dp", None, None),
            P(None, "mem"),
            P(None, "mem"),
            P(None, "mem"),
            P("mem"),
            P("dp", "mem", None),
            P("dp", "mem", None),
            P("dp", "mem", None, None),
            P("dp", "mem", None),
            P("dp", None, "mem"),
        ),
        out_specs=(P("dp", None, "mem"), P("dp", "mem"), P("dp", "mem"), P("dp", "mem"), P("mem")),
        check_vma=False,
    )
```
